32 devices in a mesh: rep: 8 (over y, x, core), sp: 4 (over z).
Axes of the slice: x: 2, y: 2, z: 4, core: 2. Of those that a mesh axis runs over, the one named last changes fastest.
Arguments:
- field: bfloat16 [8, 128, 100, 128], P('rep', 'sp'), may hold values from -6 to 6
- send_blocks: int32 [4, 4, 8], P('sp'), may hold values from 0 to 31
- send_count: int32 [4, 4], P('sp'), may hold values from 1 to 8, as said below
- regrid_weights: bfloat16 [32, 8, 128, 128], P('sp'), may hold values from -0.1875 to 0.1875
- tile_slot: int32 [32, 8], P('sp'), may hold values from 0 to 31
- edge_inputs: bfloat16 [12288, 1536], P(('rep', 'sp')), may hold values from -6 to 6
- cotangent: bfloat16 [12288, 512], P(('rep', 'sp')), may hold values from -0.15625 to 0.15625
Outputs:
- hidden: bfloat16 [8, 32, 100, 128], P('rep', 'sp')
- weight_grad: float32 [1536, 512], P(('rep', 'sp'))
The draws below stay inside these ranges and needn't reach their ends.
Inputs may be any that keep to these rules, and one draw needn't show every extreme that they name: `send_count`: every count is at most 8, and some pair of shards has exactly 8 in every draw.
All inputs are finite; a program needn't handle non-finite values.
Results may differ from the reference program's by a relative error of at most 0.001.
Values may be sent and summed in bfloat16 or wider, within the bound.
No kernel may reach another device: no remote copies, remote signals or barrier semaphores. Data moves between devices by JAX's collectives and lax.ppermute only.
A program may use at most 64 MiB of HBM per device.

```python
import jax
import jax.numpy as jnp
from jax import lax

CHANNELS = 100
HID = 512
BLK = 128
NODE_TILE = 128
READS = 8
BLOCKS_DEV = 32
PER = 8
EDGE_DEV = 384
SHARDS = 4
REPLICAS = 8
BLOCKS = 128
TILES = 32
SLOTS = 32
IN = 1536
EDGES = 12288
N_REP = 8
N_SP = 4


def draw_send_count(key, part):
    base_key = jax.random.fold_in(key, 11)
    first_key, second_key = jax.random.split(base_key)
    counts = jax.random.randint(first_key, (SHARDS * SHARDS,), 1, PER + 1)
    chosen = jax.random.randint(second_key, (), 0, SHARDS * SHARDS)
    counts = jnp.where(jnp.arange(SHARDS * SHARDS) == chosen, PER, counts)
    return counts.reshape(SHARDS, SHARDS).astype(jnp.int32)


def with_ends(array, stream_key, smallest, largest):
    shape = array.shape
    place = [jax.random.randint(jax.random.fold_in(stream_key, axis), (), 0, shape[axis]) for axis in range(len(shape))]
    array = array.at[tuple(place)].set(smallest)
    longest = shape.index(max(shape))
    place[longest] = (place[longest] + 1) % shape[longest]
    return array.at[tuple(place)].set(largest)


def raised(entries, key, source, target, blocks, factor):
    def block_of(position):
        return (jnp.arange(entries.shape[position]) // (entries.shape[position] // blocks)).reshape((-1,) + (1,) * (entries.ndim - 1 - position))

    one_side = jax.random.permutation(key, blocks)[block_of(target)]
    second = (block_of(target) + blocks // 2) % blocks
    return jnp.where((block_of(source) == one_side) | (block_of(source) == second), factor * entries, entries)


def levels(key, dims, cuts, smallest, high):
    factor_of, own = 1.0, jax.random.fold_in(key, 6)
    for axis_at, shards_of in cuts:
        draws = jnp.exp(jax.random.uniform(jax.random.fold_in(own, axis_at), (shards_of,), jnp.float32, smallest / len(cuts), high / len(cuts)))
        factor_of = factor_of * jnp.repeat(draws, dims[axis_at] // shards_of).reshape([-1 if axis == axis_at else 1 for axis in range(len(dims))])
    return factor_of


def gaussian(key, dims, width, reach, cuts=(), kind=jnp.bfloat16):
    values = jax.random.normal(key, dims, jnp.float32) * width
    if len(cuts) > 0:
        values = levels(key, dims, cuts, -0.22, 0.18) * values
    return jnp.clip(values, min=-reach, max=reach).astype(kind)


def gaussian_with(rng, dims, scale, bound, cuts, heavy, kind=jnp.bfloat16):
    drawn = scale * jax.random.normal(rng, dims, jnp.float32)
    if cuts:
        drawn = drawn * levels(rng, dims, cuts, -0.22, 0.18)
    return jnp.clip(raised(drawn, jax.random.fold_in(rng, 3), *heavy), -bound, bound).astype(kind)


def setup_inputs(seed: int = 0) -> dict:
    key_of = jax.random.split(jax.random.key(seed), 8)
    return {
        "field": gaussian(key_of[0], (REPLICAS, BLOCKS, CHANNELS, BLK), 1.0, 6.0, ((0, 8), (1, 4))),
        "send_blocks": with_ends(jax.random.randint(key_of[1], (SHARDS, SHARDS, PER), 0, BLOCKS_DEV), jax.random.fold_in(key_of[1], 1), 0, BLOCKS_DEV - 1).astype(jnp.int32),
        "send_count": draw_send_count(jax.random.fold_in(key_of[7], 71), 0),
        "regrid_weights": gaussian(key_of[3], (TILES, READS, BLK, NODE_TILE), (READS * BLK) ** -0.5, 0.1875, ((0, 4),)),
        "tile_slot": with_ends(jax.random.randint(key_of[4], (TILES, READS), 0, SLOTS), jax.random.fold_in(key_of[4], 1), 0, SLOTS - 1).astype(jnp.int32),
        "edge_inputs": gaussian_with(key_of[5], (EDGES, IN), 1.0, 6.0, ((0, 32),), (0, 1, 32, 2.75)),
        "cotangent": gaussian(key_of[6], (EDGES, HID), (EDGE_DEV * N_SP) ** -0.5, 0.15625, ((0, 32),)),
    }


def reference(field, send_blocks, send_count, regrid_weights, tile_slot, edge_inputs, cotangent):
    shards = send_blocks.shape[0]
    slots_each = send_blocks.shape[2]
    blocks_dev = field.shape[1] // shards
    tiles_dev = tile_slot.shape[0] // shards
    reads = tile_slot.shape[1]
    source = jnp.arange(shards, dtype=jnp.int32)
    global_block = source[:, None, None] * blocks_dev + send_blocks
    alive_mask = jnp.arange(slots_each, dtype=jnp.int32)[None, None, :] < send_count[:, :, None]
    global_block = jnp.transpose(global_block, (1, 0, 2)).reshape(shards, shards * slots_each)
    alive_mask = jnp.transpose(alive_mask, (1, 0, 2)).reshape(shards, shards * slots_each)
    slot_index = tile_slot.reshape(shards, tiles_dev, reads)
    weight_tiles = regrid_weights.reshape(shards, tiles_dev, reads, BLK, NODE_TILE)

    def one_sample(sample):
        def one_shard(pieces):
            blocks_read, alive, slots, weights = pieces
            received = jnp.where(alive[:, None, None], sample[blocks_read], jnp.zeros((), jnp.bfloat16))
            picked = received[slots]
            result = jnp.einsum("tbcx,tbxn->tcn", picked.astype(jnp.float32), weights.astype(jnp.float32))
            return result.astype(jnp.bfloat16)

        outcome = lax.map(one_shard, (global_block, alive_mask, slot_index, weight_tiles))
        return outcome.reshape(shards * tiles_dev, CHANNELS, NODE_TILE)

    hidden = lax.map(one_sample, field)

    groups = N_REP * N_SP
    edge_groups = edge_inputs.reshape(groups, edge_inputs.shape[0] // groups, edge_inputs.shape[1])
    cot_groups = cotangent.reshape(groups, cotangent.shape[0] // groups, cotangent.shape[1])

    def accumulate(carry, pieces):
        left, right = pieces
        product = lax.dot_general(left, right, (((0,), (0,)), ((), ())), preferred_element_type=jnp.float32)
        return carry + product, None

    start_grad = jnp.zeros((edge_inputs.shape[1], cotangent.shape[1]), jnp.float32)
    weight_grad, unused = lax.scan(accumulate, start_grad, (edge_groups, cot_groups))
    return hidden, weight_grad
```

```python
import jax
import jax.numpy as jnp
from jax import lax
from jax.sharding import Mesh, PartitionSpec as P


def body(field, send_blocks, send_count, regrid_weights, tile_slot, edge_inputs, cotangent):
    sample = field[0]
    own_lists = send_blocks[0]
    shards = own_lists.shape[0]
    slots_each = own_lists.shape[1]
    channels = sample.shape[1]
    cells = sample.shape[2]
    groups = lax.axis_size("group")
    alive = jnp.arange(slots_each, dtype=jnp.int32)[None, :] < send_count[0][:, None]
    outgoing = jnp.where(alive[:, :, None, None], sample[own_lists], jnp.zeros((), jnp.bfloat16))
    incoming = lax.all_to_all(outgoing, "sp", split_axis=0, concat_axis=0, tiled=True)

    partial_grad = lax.dot_general(
        edge_inputs, cotangent, (((0,), (0,)), ((), ())), preferred_element_type=jnp.float32
    )
    rows = partial_grad.shape[0] // (groups * 2 * shards)
    hid = partial_grad.shape[1]
    halves = partial_grad.reshape(groups, 2, shards * rows, hid)
    first = lax.axis_index("pair") == 0
    keep = jnp.where(first, halves[:, 0], halves[:, 1])
    give = jnp.where(first, halves[:, 1], halves[:, 0])
    pair_sum = keep + lax.ppermute(give, "pair", [(0, 1), (1, 0)])
    shift = jnp.clip(14.0 - jnp.ceil(jnp.log2(jnp.max(jnp.abs(pair_sum)))), -100.0, 100.0)
    scaled = (pair_sum * jnp.exp2(shift)).astype(jnp.float16)
    scaled = scaled.reshape(groups * shards, rows, hid)
    tag = jnp.full((groups * shards, 1, hid), shift.astype(jnp.float16))
    received = lax.all_to_all(
        jnp.concatenate([scaled, tag], axis=1), ("group", "sp"), split_axis=0, concat_axis=0, tiled=True
    )
    unscale = jnp.exp2(-received[:, rows:, :].astype(jnp.float32))
    weight_grad = jnp.sum(received[:, :rows].astype(jnp.float32) * unscale, axis=0)

    block_pool = incoming.reshape(shards * slots_each, channels, cells)
    picked = block_pool[tile_slot]
    hidden = jnp.einsum(
        "tbcx,tbxn->tcn", picked, regrid_weights, preferred_element_type=jnp.float32
    )
    hidden = hidden.astype(jnp.bfloat16)[None]
    return (hidden, weight_grad)


def solution(mesh):
    split = Mesh(
        mesh.devices.reshape(mesh.shape["rep"] // 2, 2, mesh.shape["sp"]), ("group", "pair", "sp")
    )
    rep = ("group", "pair")
    in_specs = (
        P(rep, "sp", None, None),
        P("sp", None, None),
        P("sp", None),
        P("sp", None, None, None),
        P("sp", None),
        P((*rep, "sp"), None),
        P((*rep, "sp"), None),
    )
    out_specs = (P(rep, "sp", None, None), P((*rep, "sp"), None))
    return jax.shard_map(body, mesh=split, in_specs=in_specs, out_specs=out_specs, check_vma=False)
```

```python
import jax
import jax.numpy as jnp
from jax import lax
from jax.sharding import Mesh, PartitionSpec as P


def power_of_two_shift(values):
    return jnp.clip(14.0 - jnp.ceil(jnp.log2(jnp.max(jnp.abs(values)))), -100.0, 100.0)


def pack(values, shift):
    scaled = (values * jnp.exp2(shift)).astype(jnp.float16)
    pad = [(0, 0, 0)] * (values.ndim - 2) + [(0, 1, 0), (0, 0, 0)]
    return lax.pad(scaled, shift.astype(jnp.float16), pad)


def unpack(received):
    unscale = jnp.exp2(-received[..., -1:, :].astype(jnp.float32))
    return received[..., :-1, :].astype(jnp.float32) * unscale


def body(field, send_blocks, send_count, regrid_weights, tile_slot, edge_inputs, cotangent):
    sample = field[0]
    own_lists = send_blocks[0]
    shards = own_lists.shape[0]
    slots_each = own_lists.shape[1]
    groups = lax.axis_size("group")
    place = lax.axis_index("sp")

    def to_shift(k):
        return [(i, (i + k) % shards) for i in range(shards)]

    outgoing = []
    for k in range(shards):
        dest = (place + k) % shards
        alive = jnp.arange(slots_each, dtype=jnp.int32) < send_count[0, dest]
        outgoing.append(
            jnp.where(alive[:, None, None], sample[own_lists[dest]], jnp.zeros((), jnp.bfloat16))
        )
    edge_inputs, cotangent, *outgoing = lax.optimization_barrier((edge_inputs, cotangent, *outgoing))
    incoming = [outgoing[0]] + [
        lax.ppermute(outgoing[k], "sp", to_shift(k)) for k in range(1, shards)
    ]

    partial_grad = lax.dot_general(
        edge_inputs, cotangent, (((0,), (0,)), ((), ())), preferred_element_type=jnp.float32
    )
    rows = partial_grad.shape[0] // (groups * 2 * shards)
    hid = partial_grad.shape[1]
    halves = partial_grad.reshape(groups, 2, shards * rows, hid)
    first = lax.axis_index("pair") == 0
    keep = jnp.where(first, halves[:, 0], halves[:, 1])
    give = jnp.where(first, halves[:, 1], halves[:, 0])
    pair_sum = keep + lax.ppermute(give, "pair", [(0, 1), (1, 0)])
    received = lax.all_to_all(
        pack(pair_sum, power_of_two_shift(pair_sum)), "group", split_axis=0, concat_axis=0, tiled=True
    )
    rep_sum = jnp.sum(unpack(received), axis=0).reshape(shards, rows, hid)
    shift = power_of_two_shift(rep_sum)
    weight_grad = lax.dynamic_index_in_dim(rep_sum, place, 0, keepdims=False)
    for k in range(1, shards):
        chunk = lax.dynamic_index_in_dim(rep_sum, (place + k) % shards, 0, keepdims=False)
        weight_grad = weight_grad + unpack(lax.ppermute(pack(chunk, shift), "sp", to_shift(k)))

    block_pool = jnp.concatenate(incoming, axis=0)
    source = tile_slot // slots_each
    slot = (place - source) % shards * slots_each + tile_slot % slots_each
    hidden = jnp.einsum(
        "tbcx,tbxn->tcn", block_pool[slot], regrid_weights, preferred_element_type=jnp.float32
    )
    hidden = hidden.astype(jnp.bfloat16)[None]
    return (hidden, weight_grad)


def solution(mesh):
    split = Mesh(
        mesh.devices.reshape(mesh.shape["rep"] // 2, 2, mesh.shape["sp"]), ("group", "pair", "sp")
    )
    rep = ("group", "pair")
    in_specs = (
        P(rep, "sp", None, None),
        P("sp", None, None),
        P("sp", None),
        P("sp", None, None, None),
        P("sp", None),
        P((*rep, "sp"), None),
        P((*rep, "sp"), None),
    )
    out_specs = (P(rep, "sp", None, None), P((*rep, "sp"), None))
    return jax.shard_map(body, mesh=split, in_specs=in_specs, out_specs=out_specs, check_vma=False)
```

```python
import jax
import jax.numpy as jnp
from jax import lax
from jax.sharding import Mesh, PartitionSpec as P


def power_of_two_shift(values):
    return jnp.clip(14.0 - jnp.ceil(jnp.log2(jnp.max(jnp.abs(values)))), -100.0, 100.0)


def pack(values, shift):
    scaled = (values * jnp.exp2(shift)).astype(jnp.float16)
    tag = jnp.broadcast_to(shift.astype(jnp.float16), values.shape[:-2] + (1, values.shape[-1]))
    return jnp.concatenate([scaled, tag], axis=-2)


def unpack(received):
    unscale = jnp.exp2(-received[..., -1:, :].astype(jnp.float32))
    return received[..., :-1, :].astype(jnp.float32) * unscale


def work(field, send_blocks, send_count, regrid_weights, tile_slot, edge_inputs, cotangent):
    sample = field[0]
    own_lists = send_blocks[0]
    shards = own_lists.shape[0]
    slots_each = own_lists.shape[1]
    groups = lax.axis_size("group")
    place = lax.axis_index("sp")

    def to_shift(k):
        return [(i, (i + k) % shards) for i in range(shards)]

    k_dest = (place + jnp.arange(shards, dtype=jnp.int32)) % shards
    pick_dest = k_dest[:, None] == jnp.arange(shards, dtype=jnp.int32)[None, :]
    alive = jnp.arange(slots_each, dtype=jnp.int32)[None, :] < send_count[0][:, None]
    live_list = jnp.where(alive, own_lists, -1)
    rolled = jnp.sum(jnp.where(pick_dest[:, :, None], live_list[None], 0), axis=1)
    blocks = jnp.arange(sample.shape[0], dtype=jnp.int32)
    choose = (rolled[:, :, None] == blocks).astype(jnp.bfloat16)
    outgoing = jnp.einsum("kjb,bcx->kjcx", choose, sample, preferred_element_type=jnp.bfloat16)
    incoming = [outgoing[0]] + [
        lax.ppermute(outgoing[k], "sp", to_shift(k)) for k in range(1, shards)
    ]

    partial_grad = lax.dot_general(edge_inputs, cotangent, (((0,), (0,)), ((), ())), preferred_element_type=jnp.float32)
    rows = partial_grad.shape[0] // (groups * 2 * shards)
    hid = partial_grad.shape[1]
    halves = partial_grad.reshape(groups, 2, shards * rows, hid)
    first = lax.axis_index("pair") == 0
    keep = jnp.where(first, halves[:, 0], halves[:, 1])
    give = jnp.where(first, halves[:, 1], halves[:, 0])
    pair_sum = keep + lax.ppermute(give, "pair", [(0, 1), (1, 0)])
    received = lax.all_to_all(
        pack(pair_sum, power_of_two_shift(pair_sum)), "group", split_axis=0, concat_axis=0, tiled=True
    )
    rep_sum = jnp.sum(unpack(received), axis=0).reshape(shards, rows, hid)
    shift = jnp.min(received[:, -1, :].astype(jnp.float32), axis=0) - float((groups - 1).bit_length())
    shift = shift[None, :]
    weight_grad = lax.dynamic_index_in_dim(rep_sum, place, 0, keepdims=False)
    for k in range(1, shards):
        chunk = lax.dynamic_index_in_dim(rep_sum, (place + k) % shards, 0, keepdims=False)
        weight_grad = weight_grad + unpack(lax.ppermute(pack(chunk, shift), "sp", to_shift(k)))

    block_pool = jnp.concatenate(incoming, axis=0)
    source = tile_slot // slots_each
    slot = (place - source) % shards * slots_each + tile_slot % slots_each
    hidden = jnp.einsum(
        "tbcx,tbxn->tcn", block_pool[slot], regrid_weights, preferred_element_type=jnp.float32
    )
    hidden = hidden.astype(jnp.bfloat16)[None]
    return (hidden, weight_grad)


def solution(mesh):
    split = Mesh(
        mesh.devices.reshape(mesh.shape["rep"] // 2, 2, mesh.shape["sp"]), ("group", "pair", "sp")
    )
    rep = ("group", "pair")
    in_specs = (
        P(rep, "sp", None, None),
        P("sp", None, None),
        P("sp", None),
        P("sp", None, None, None),
        P("sp", None),
        P((*rep, "sp"), None),
        P((*rep, "sp"), None),
    )
    out_specs = (P(rep, "sp", None, None), P((*rep, "sp"), None))
    return jax.shard_map(work, mesh=split, in_specs=in_specs, out_specs=out_specs, check_vma=False)
```

```python
import jax
import jax.numpy as jnp
from jax import lax
from jax.sharding import Mesh, PartitionSpec as P


def power_of_two_shift(bound):
    return jnp.clip(14.0 - jnp.ceil(jnp.log2(bound)), -100.0, 100.0)


def pack(values, shift):
    scaled = (values * jnp.exp2(shift)).astype(jnp.float16)
    tag = jnp.broadcast_to(shift.astype(jnp.float16), values.shape[:-2] + (1, values.shape[-1]))
    return jnp.concatenate([scaled, tag], axis=-2)


def unpack(received):
    unscale = jnp.exp2(-received[..., -1:, :].astype(jnp.float32))
    return received[..., :-1, :].astype(jnp.float32) * unscale


def work(field, send_blocks, send_count, regrid_weights, tile_slot, edge_inputs, cotangent):
    sample = field[0]
    own_lists = send_blocks[0]
    shards = own_lists.shape[0]
    slots_each = own_lists.shape[1]
    groups = lax.axis_size("group")
    place = lax.axis_index("sp")

    def to_shift(k):
        return [(i, (i + k) % shards) for i in range(shards)]

    k_dest = (place + jnp.arange(shards, dtype=jnp.int32)) % shards
    pick_dest = k_dest[:, None] == jnp.arange(shards, dtype=jnp.int32)[None, :]
    alive = jnp.arange(slots_each, dtype=jnp.int32)[None, :] < send_count[0][:, None]
    live_list = jnp.where(alive, own_lists, -1)
    rolled = jnp.sum(jnp.where(pick_dest[:, :, None], live_list[None], 0), axis=1)
    blocks = jnp.arange(sample.shape[0], dtype=jnp.int32)
    choose = (rolled[:, :, None] == blocks).astype(jnp.bfloat16)
    outgoing = jnp.einsum("kjb,bcx->kjcx", choose, sample, preferred_element_type=jnp.bfloat16)
    incoming = [outgoing[0]] + [
        lax.ppermute(outgoing[k], "sp", to_shift(k)) for k in range(1, shards)
    ]

    partial_grad = lax.dot_general(
        edge_inputs, cotangent, (((0,), (0,)), ((), ())), preferred_element_type=jnp.float32
    )
    rows = partial_grad.shape[0] // (groups * 2 * shards)
    hid = partial_grad.shape[1]
    halves = partial_grad.reshape(groups, 2, shards * rows, hid)
    first = lax.axis_index("pair") == 0
    keep = jnp.where(first, halves[:, 0], halves[:, 1])
    give = jnp.where(first, halves[:, 1], halves[:, 0])
    keep, give = lax.optimization_barrier((keep, give))
    swap = [(0, 1), (1, 0)]
    taken = lax.ppermute(give, "pair", swap)
    own_max = jnp.max(jnp.maximum(jnp.abs(keep), jnp.abs(give)), axis=(0, 1))[None, :]
    bound = own_max + lax.ppermute(own_max, "pair", swap)
    packed = pack(keep + taken, power_of_two_shift(bound)[None])
    received = lax.all_to_all(packed, "group", split_axis=0, concat_axis=0, tiled=True)
    rep_sum = jnp.sum(unpack(received), axis=0).reshape(shards, rows, hid)
    shift = jnp.min(received[:, -1, :].astype(jnp.float32), axis=0) - float((groups - 1).bit_length())
    shift = shift[None, :]
    weight_grad = lax.dynamic_index_in_dim(rep_sum, place, 0, keepdims=False)
    for k in range(1, shards):
        chunk = lax.dynamic_index_in_dim(rep_sum, (place + k) % shards, 0, keepdims=False)
        weight_grad = weight_grad + unpack(lax.ppermute(pack(chunk, shift), "sp", to_shift(k)))

    block_pool = jnp.concatenate(incoming, axis=0)
    source = tile_slot // slots_each
    slot = (place - source) % shards * slots_each + tile_slot % slots_each
    hidden = jnp.einsum(
        "tbcx,tbxn->tcn", block_pool[slot], regrid_weights, preferred_element_type=jnp.float32
    )
    hidden = hidden.astype(jnp.bfloat16)[None]
    return (hidden, weight_grad)


def solution(mesh):
    split = Mesh(
        mesh.devices.reshape(mesh.shape["rep"] // 2, 2, mesh.shape["sp"]), ("group", "pair", "sp")
    )
    rep = ("group", "pair")
    in_specs = (
        P(rep, "sp", None, None),
        P("sp", None, None),
        P("sp", None),
        P("sp", None, None, None),
        P("sp", None),
        P((*rep, "sp"), None),
        P((*rep, "sp"), None),
    )
    out_specs = (P(rep, "sp", None, None), P((*rep, "sp"), None))
    return jax.shard_map(work, mesh=split, in_specs=in_specs, out_specs=out_specs, check_vma=False)
```

```python
import jax
import jax.numpy as jnp
from jax import lax
from jax.sharding import Mesh, PartitionSpec as P


def power_of_two_shift(bound):
    return jnp.clip(14.0 - jnp.ceil(jnp.log2(bound)), -100.0, 100.0)


def pack(values, shift):
    scaled = (values * jnp.exp2(shift)).astype(jnp.float16)
    tag = jnp.broadcast_to(shift.astype(jnp.float16), values.shape[:-2] + (1, values.shape[-1]))
    return jnp.concatenate([scaled, tag], axis=-2)


def unpack(received):
    unscale = jnp.exp2(-received[..., -1:, :].astype(jnp.float32))
    return received[..., :-1, :].astype(jnp.float32) * unscale


def work(field, send_blocks, send_count, regrid_weights, tile_slot, edge_inputs, cotangent):
    sample = field[0]
    own_lists = send_blocks[0]
    shards = own_lists.shape[0]
    slots_each = own_lists.shape[1]
    groups = lax.axis_size("group")
    place = lax.axis_index("sp")

    def to_shift(k):
        return [(i, (i + k) % shards) for i in range(shards)]

    k_dest = (place + jnp.arange(shards, dtype=jnp.int32)) % shards
    pick_dest = k_dest[:, None] == jnp.arange(shards, dtype=jnp.int32)[None, :]
    alive = jnp.arange(slots_each, dtype=jnp.int32)[None, :] < send_count[0][:, None]
    live_list = jnp.where(alive, own_lists, -1)
    rolled = jnp.sum(jnp.where(pick_dest[:, :, None], live_list[None], 0), axis=1)
    blocks = jnp.arange(sample.shape[0], dtype=jnp.int32)
    choose = (rolled[:, :, None] == blocks).astype(jnp.bfloat16)
    outgoing = jnp.einsum("kjb,bcx->kjcx", choose, sample, preferred_element_type=jnp.bfloat16)
    incoming = [outgoing[0]]
    for k in range(1, shards):
        incoming.append(lax.ppermute(outgoing[k], "sp", to_shift(k)))

    partial_grad = lax.dot_general(
        edge_inputs, cotangent, (((0,), (0,)), ((), ())), preferred_element_type=jnp.float32
    )
    rows = partial_grad.shape[0] // (groups * 2 * shards)
    hid = partial_grad.shape[1]
    halves = partial_grad.reshape(groups, 2, shards * rows, hid)
    first = lax.axis_index("pair") == 0
    keep = jnp.where(first, halves[:, 0], halves[:, 1])
    give = jnp.where(first, halves[:, 1], halves[:, 0])
    keep, give = lax.optimization_barrier((keep, give))
    swap = [(0, 1), (1, 0)]
    taken = lax.ppermute(give, "pair", swap)
    own_max = jnp.max(jnp.maximum(jnp.abs(keep), jnp.abs(give)), axis=(0, 1))[None, :]
    bound = own_max + lax.ppermute(own_max, "pair", swap)
    packed = pack(keep + taken, power_of_two_shift(bound)[None])
    received = lax.all_to_all(packed, "group", split_axis=0, concat_axis=0, tiled=True)
    rep_sum = jnp.sum(unpack(received), axis=0).reshape(shards, rows, hid)
    shift = jnp.min(received[:, -1, :].astype(jnp.float32), axis=0) - float((groups - 1).bit_length())
    shift = shift[None, :]
    weight_grad = lax.dynamic_index_in_dim(rep_sum, place, 0, keepdims=False)
    for k in range(1, shards):
        chunk = lax.dynamic_index_in_dim(rep_sum, (place + k) % shards, 0, keepdims=False)
        weight_grad = weight_grad + unpack(lax.ppermute(pack(chunk, shift), "sp", to_shift(k)))

    block_pool = jnp.concatenate(incoming, axis=0)
    source = tile_slot // slots_each
    slot = (place - source) % shards * slots_each + tile_slot % slots_each
    hidden = jnp.einsum(
        "tbcx,tbxn->tcn", block_pool[slot], regrid_weights, preferred_element_type=jnp.float32
    )
    hidden = hidden.astype(jnp.bfloat16)[None]
    return (hidden, weight_grad)


def solution(mesh):
    split = Mesh(
        mesh.devices.reshape(mesh.shape["rep"] // 2, 2, mesh.shape["sp"]), ("group", "pair", "sp")
    )
    rep = ("group", "pair")
    in_specs = (
        P(rep, "sp", None, None),
        P("sp", None, None),
        P("sp", None),
        P("sp", None, None, None),
        P("sp", None),
        P((*rep, "sp"), None),
        P((*rep, "sp"), None),
    )
    out_specs = (P(rep, "sp", None, None), P((*rep, "sp"), None))
    return jax.shard_map(work, mesh=split, in_specs=in_specs, out_specs=out_specs, check_vma=False)
```
